32 devices in a mesh: groups: 1, role: 2 (over core), ep: 8 (over z, y), tp: 2 (over x).
Axes of the slice: x: 2, y: 2, z: 4, core: 2. Of those that a mesh axis runs over, the one named last changes fastest.
Arguments:
- tokens: bfloat16 [2048, 2048], P(('groups', 'role', 'ep'), 'tp'), may hold values from -6 to 6
- out_grad: bfloat16 [2048, 2048], P(('groups', 'role', 'ep'), 'tp'), may hold values from -6 to 6
- routes: int32 [2048, 8], P(('groups', 'role', 'ep')), may hold values from 0 to 15, all different within a row; in each aligned block of 128 rows (0 to 127, 128 to 255, ...) at most 72 rows name the same one
- probs: bfloat16 [2048, 8], P(('groups', 'role', 'ep')), may hold values from 0.049804688 to 1
- w_gate: bfloat16 [16, 2048, 768], P(('role', 'ep'), None, 'tp'), may hold values from -0.125 to 0.125
- w_up: bfloat16 [16, 2048, 768], P(('role', 'ep'), None, 'tp'), may hold values from -0.125 to 0.125
- w_down: bfloat16 [16, 768, 2048], P(('role', 'ep'), 'tp'), may hold values from -0.21875 to 0.21875
Outputs:
- d_tokens: bfloat16 [2048, 2048], P(('groups', 'role', 'ep'), 'tp')
- d_probs: float32 [2048, 8], P(('groups', 'role', 'ep'))
- d_w_gate: bfloat16 [16, 2048, 768], P(('groups', 'role', 'ep'), None, 'tp')
- d_w_up: bfloat16 [16, 2048, 768], P(('groups', 'role', 'ep'), None, 'tp')
- d_w_down: bfloat16 [16, 768, 2048], P(('groups', 'role', 'ep'), 'tp')
The draws below stay inside these ranges and needn't reach their ends.
Inputs may be any that keep to these rules, and one draw needn't show every extreme that they name: `routes`: in each aligned block of 128 rows (the tokens of one index of role and ep) no expert is named by more than 72 rows, a bound that some block reaches.
All inputs are finite; a program needn't handle non-finite values.
Results may differ from the reference program's by a relative error of at most 0.012.
Values may be sent and summed in bfloat16 or wider, within the bound.
A program may use at most 128 MiB of HBM per device.

```python
import math
import jax
import jax.numpy as jnp
import numpy as np
from jax import lax

D = 2048
HIDDEN_SIZE = 768
TOP = 8
TOK_DEV = 128
EXPERTS = 16
CAP = 72
TOKENS = 2048
N_TP = 2


def levels(rng, dims, cuts, smallest, largest):
    loudness = 1.0
    for position, parts in cuts:
        heights = jax.random.uniform(jax.random.fold_in(jax.random.fold_in(rng, 6), position), (parts,), jnp.float32, smallest / len(cuts), largest / len(cuts))
        loudness = loudness * jnp.repeat(jnp.exp(heights), dims[position] // parts).reshape((-1,) + (1,) * (len(dims) - 1 - position))
    return loudness


def routed_block(rng, own, number, rows, amount, top, bound, lean):
    ranking = jax.random.permutation(rng, amount)
    crowded, usual = load_shares(amount, rows * top, bound, lean, True), load_shares(amount, rows * top, bound, lean, False)
    places = jnp.arange(amount)

    def named(lengths, rotation):
        used = int((lengths > 0).sum())
        fixed = max(1, used // 4)
        moved = fixed + (places - fixed + rotation * (used - fixed)) % max(1, amount - fixed)
        return jnp.zeros((amount,), jnp.int32).at[ranking[jnp.where(places < fixed, places, moved)]].set(jnp.asarray(lengths, jnp.int32))

    lengths = jnp.where(number % 4 == 0, named(crowded, number // 4), named(usual, number - number // 4 - 1))
    mixed = jax.random.permutation(jax.random.fold_in(own, 3), amount)
    giver, taker = mixed[0:amount // 2 * 2:2], mixed[1:amount // 2 * 2:2]
    room = jnp.minimum(lengths[giver] - 1, bound - lengths[taker]) // 2
    room = jnp.where((giver == ranking[0]) | (taker == ranking[0]) | (lengths[taker] == 0), 0, jnp.maximum(room, 0))
    moved = jax.random.randint(jax.random.fold_in(own, 4), (amount // 2,), 0, 1 << 20) % (room + 1)
    lengths = lengths.at[giver].add(-moved).at[taker].add(moved)
    labels = jnp.searchsorted(jnp.cumsum(lengths), jnp.arange(rows * top), side="right").astype(jnp.int32)
    table = labels.reshape(top, rows).T
    table = table[jax.random.permutation(jax.random.fold_in(own, 1), rows)]
    rotation = jax.random.randint(jax.random.fold_in(own, 2), (rows, 1), 0, top)
    return jnp.take_along_axis(table, (jnp.arange(top)[None, :] + rotation) % top, axis=1)


def load_shares(amount, total, bound, lean, full):
    loads = [(1 << 20) // math.isqrt(standing ** lean) + 1 for standing in range(1, amount + 1)]
    largest = bound if full else min(bound, max(-(-total // amount), total * loads[0] // sum(loads)))
    least = 1 if total - largest >= amount - 1 else 0
    holding, surplus = [largest] + [least] * (amount - 1), total - largest - least * (amount - 1)
    while surplus > 0:
        candidates = [i for i in range(1, amount) if holding[i] < largest] or [i for i in range(1, amount) if holding[i] < bound]
        pool, budget = sum([loads[i] for i in candidates]), surplus
        for i in candidates:
            addition = min(bound - holding[i], max(1, budget * loads[i] // pool), surplus)
            holding[i] = holding[i] + addition
            surplus = surplus - addition
    return np.array(holding)


def gaussian(stream_key, dims, scale, reach, cuts=(), held_as=jnp.bfloat16):
    result = scale * jax.random.normal(stream_key, dims, jnp.float32)
    if cuts:
        result = result * levels(stream_key, dims, cuts, -0.22, 0.18)
    return jnp.clip(result, -reach, reach).astype(held_as)


def setup_inputs(seed: int = 0, part: int = 0) -> dict:
    splits = jax.random.split(jax.random.key(seed), 8)
    own_keys = jax.random.split(jax.random.fold_in(splits[7], part), 8)
    tokens = gaussian(own_keys[0], (TOKENS, D), 1.0, 6.0, ((0, 16), (1, 2)))
    out_grad = gaussian(own_keys[1], (TOKENS, D), 1.0, 6.0, ((0, 16), (1, 2)))
    routes_keys = jax.random.split(jax.random.fold_in(own_keys[2], 1), TOKENS // TOK_DEV)
    routes_turns = jax.random.permutation(jax.random.fold_in(own_keys[2], 3), TOKENS // TOK_DEV)
    routes = jax.vmap(lambda own, number: routed_block(jax.random.fold_in(own_keys[2], 2), own, number, TOK_DEV, EXPERTS, TOP, CAP, 2))(routes_keys, routes_turns).reshape((TOKENS, TOP))
    probs = jnp.clip(jnp.exp(math.log(1.0) - 2.9996462 * jax.random.uniform(own_keys[3], (TOKENS, TOP), jnp.float32) ** levels(own_keys[3], (TOKENS, TOP), ((0, 16),), -0.2, 0.2)), 0.049804688, 1.0).astype(jnp.bfloat16)
    w_gate = gaussian(splits[4], (EXPERTS, D, HIDDEN_SIZE), D ** -0.5, 0.125, ((0, 16), (2, 2)))
    w_up = gaussian(splits[5], (EXPERTS, D, HIDDEN_SIZE), D ** -0.5, 0.125, ((0, 16), (2, 2)))
    w_down = gaussian(splits[6], (EXPERTS, HIDDEN_SIZE, D), HIDDEN_SIZE ** -0.5, 0.21875, ((0, 16), (1, 2)))
    return {"tokens": tokens, "out_grad": out_grad, "routes": routes, "probs": probs, "w_gate": w_gate, "w_up": w_up, "w_down": w_down}


HIGHEST_PRECISION = lax.Precision.HIGHEST


def reference(tokens, out_grad, routes, probs, w_gate, w_up, w_down):
    total_rows = tokens.shape[0]
    width_full = tokens.shape[1]
    blocks = total_rows // TOK_DEV
    length = TOK_DEV * TOP
    routes_block = routes.reshape(blocks, length)
    onehot = (routes_block[:, :, None] == jnp.arange(EXPERTS, dtype=jnp.int32)[None, None, :]).astype(jnp.int32)
    before = jnp.cumsum(onehot, axis=1) - onehot
    slot_index = jnp.sum(before * onehot, axis=2).reshape(-1).astype(jnp.int32)
    owner_ids = routes_block.reshape(-1).astype(jnp.int32)
    source = jnp.repeat(jnp.arange(blocks, dtype=jnp.int32), length)
    entries = jnp.arange(blocks * length, dtype=jnp.int32)
    slot_table = jnp.full((EXPERTS, blocks, CAP), blocks * length, jnp.int32)
    slot_table = slot_table.at[owner_ids, source, slot_index].set(entries)
    padded_x = jnp.concatenate([tokens.astype(jnp.float32), jnp.zeros((1, width_full), jnp.float32)], 0)
    padded_g = jnp.concatenate([out_grad.astype(jnp.float32), jnp.zeros((1, width_full), jnp.float32)], 0)
    padded_p = jnp.concatenate([probs.reshape(-1).astype(jnp.float32), jnp.zeros((1,), jnp.float32)], 0)
    hidden_size = w_gate.shape[2]
    part_size = hidden_size // N_TP

    def expert(carried, inputs):
        d_tok, d_prob = carried
        table_rows, gate_weight, up_weight, down_weight = inputs
        entry_index = table_rows.reshape(-1)
        token_index = entry_index // TOP
        rows_x = padded_x[token_index]
        rows_g = padded_g[token_index]
        weight_p = padded_p[entry_index][:, None]
        gate_f = gate_weight.astype(jnp.float32)
        up_f = up_weight.astype(jnp.float32)
        down_f = down_weight.astype(jnp.float32)
        gate_rows = jnp.dot(rows_x, gate_f, precision=HIGHEST_PRECISION)
        up_rows = jnp.dot(rows_x, up_f, precision=HIGHEST_PRECISION)
        sigmoid_gate = jax.nn.sigmoid(gate_rows)
        activated = gate_rows * sigmoid_gate
        hidden = activated * up_rows
        back_rows = jnp.dot(rows_g, down_f.T, precision=HIGHEST_PRECISION)
        scores = jnp.sum(hidden * back_rows, axis=1)
        hidden_grad = weight_p * back_rows
        d_gate_rows = (hidden_grad * up_rows * sigmoid_gate * (1.0 + gate_rows * (1.0 - sigmoid_gate))).astype(jnp.bfloat16)
        d_up_rows = (hidden_grad * activated).astype(jnp.bfloat16)
        scaled = (weight_p * hidden).astype(jnp.bfloat16)
        d_gate_rows, d_up_rows, scaled = lax.optimization_barrier((d_gate_rows, d_up_rows, scaled))
        d_gate_f = d_gate_rows.astype(jnp.float32)
        d_up_f = d_up_rows.astype(jnp.float32)
        grad_down = jnp.dot(scaled.astype(jnp.float32).T, rows_g, precision=HIGHEST_PRECISION).astype(jnp.bfloat16)
        grad_gate = jnp.dot(rows_x.T, d_gate_f, precision=HIGHEST_PRECISION).astype(jnp.bfloat16)
        grad_up = jnp.dot(rows_x.T, d_up_f, precision=HIGHEST_PRECISION).astype(jnp.bfloat16)
        row_count = entry_index.shape[0]
        gate_blocks = d_gate_f.reshape(row_count, N_TP, part_size)
        up_blocks = d_up_f.reshape(row_count, N_TP, part_size)
        gate_split = gate_f.reshape(width_full, N_TP, part_size)
        up_split = up_f.reshape(width_full, N_TP, part_size)
        pieces = jnp.einsum("rbh,dbh->rbd", gate_blocks, gate_split, precision=HIGHEST_PRECISION)
        pieces = pieces + jnp.einsum("rbh,dbh->rbd", up_blocks, up_split, precision=HIGHEST_PRECISION)
        pieces = lax.optimization_barrier(pieces.astype(jnp.bfloat16)).astype(jnp.float32)
        route_grad = lax.optimization_barrier(jnp.sum(pieces, axis=1).astype(jnp.bfloat16)).astype(jnp.float32)
        d_tok = d_tok.at[token_index].add(route_grad)
        d_prob = d_prob.at[entry_index].add(scores)
        return (d_tok, d_prob), (grad_gate, grad_up, grad_down)

    start = (jnp.zeros((total_rows + 1, width_full), jnp.float32), jnp.zeros((blocks * length + 1,), jnp.float32))
    (d_tok, d_prob), (grads_gate, grads_up, grads_down) = lax.scan(expert, start, (slot_table, w_gate, w_up, w_down))
    d_tokens = d_tok[:total_rows].astype(jnp.bfloat16)
    d_probs = d_prob[:blocks * length].reshape(total_rows, TOP)
    return (d_tokens, d_probs, grads_gate, grads_up, grads_down)
```

```python
import jax
import jax.numpy as jnp
from jax import lax
from jax.sharding import PartitionSpec as P


def pad_rows(array):
    return jnp.concatenate([array, jnp.zeros((1, array.shape[1]), array.dtype)], 0)


def routed_device(tokens, out_grad, routes, probs, w_gate, w_up, w_down):
    owners = lax.axis_size(("role", "ep"))
    tok_rows, top_count = routes.shape
    width_full = w_gate.shape[1]
    part_width = w_gate.shape[2]
    capacity = min(tok_rows, tok_rows * top_count * 9 // (8 * owners))
    entry_total = tok_rows * top_count
    routes_flat = routes.reshape(-1)
    onehot = (routes_flat[:, None] == jnp.arange(owners, dtype=jnp.int32)[None, :]).astype(
        jnp.int32
    )
    before = jnp.cumsum(onehot, axis=0) - onehot
    slot_index = jnp.sum(before * onehot, axis=1)
    target = routes_flat * capacity + slot_index
    row_count = owners * capacity
    entry_of_slot = (
        jnp.full((row_count,), entry_total, jnp.int32)
        .at[target]
        .set(jnp.arange(entry_total, dtype=jnp.int32))
    )
    token_of_slot = entry_of_slot // top_count
    padded_prob = jnp.concatenate([probs.reshape(-1), jnp.zeros((1,), probs.dtype)], 0)
    send_prob = padded_prob[entry_of_slot].reshape(owners, capacity)
    send_x = pad_rows(tokens)[token_of_slot]
    send_g = pad_rows(out_grad)[token_of_slot]
    slice_x, slice_g, recv_p = (
        lax.all_to_all(
            send_x.reshape(owners, capacity, tokens.shape[1]),
            ("role", "ep"),
            split_axis=0,
            concat_axis=0,
            tiled=True,
        ),
        lax.all_to_all(
            send_g.reshape(owners, capacity, tokens.shape[1]),
            ("role", "ep"),
            split_axis=0,
            concat_axis=0,
            tiled=True,
        ),
        lax.all_to_all(send_prob, ("role", "ep"), split_axis=0, concat_axis=0, tiled=True),
    )
    recv_x, recv_g = (
        lax.all_gather(slice_x, "tp", axis=2, tiled=True),
        lax.all_gather(slice_g, "tp", axis=2, tiled=True),
    )
    rows_x = recv_x.reshape(row_count, width_full)
    rows_g = recv_g.reshape(row_count, width_full)
    weight_p = recv_p.reshape(row_count, 1).astype(jnp.float32)
    gate_up = jnp.concatenate([w_gate[0], w_up[0]], 1)
    down_shard = w_down[0]
    both_rows = jnp.dot(rows_x, gate_up, preferred_element_type=jnp.float32)
    gate_rows = both_rows[:, :part_width]
    up_rows = both_rows[:, part_width:]
    sigmoid_gate = jax.nn.sigmoid(gate_rows)
    activated = gate_rows * sigmoid_gate
    hidden = activated * up_rows
    back_rows = lax.dot_general(
        rows_g, down_shard, (((1,), (1,)), ((), ())), preferred_element_type=jnp.float32
    )
    scores = lax.psum(jnp.sum(hidden * back_rows, axis=1), "tp")
    hidden_grad = weight_p * back_rows
    d_gate_rows = (
        hidden_grad * up_rows * sigmoid_gate * (1.0 + gate_rows * (1.0 - sigmoid_gate))
    ).astype(jnp.bfloat16)
    d_up_rows = (hidden_grad * activated).astype(jnp.bfloat16)
    d_both = jnp.concatenate([d_gate_rows, d_up_rows], 1)
    scaled = (weight_p * hidden).astype(jnp.bfloat16)
    grad_down = lax.dot_general(
        scaled, rows_g, (((0,), (0,)), ((), ())), preferred_element_type=jnp.float32
    )
    grad_both = lax.dot_general(
        rows_x, d_both, (((0,), (0,)), ((), ())), preferred_element_type=jnp.float32
    )
    grad_gate = grad_both[:, :part_width]
    grad_up = grad_both[:, part_width:]
    partial_low = lax.dot_general(
        d_both, gate_up, (((1,), (1,)), ((), ())), preferred_element_type=jnp.float32
    ).astype(jnp.bfloat16)
    home_s = lax.all_to_all(
        scores.reshape(owners, capacity), ("role", "ep"), split_axis=0, concat_axis=0, tiled=True
    )
    summed = lax.psum_scatter(
        partial_low.reshape(owners, capacity, width_full), "tp", scatter_dimension=2, tiled=True
    ).astype(jnp.float32)
    summed_low = summed.astype(jnp.bfloat16)
    home_x = lax.all_to_all(summed_low, ("role", "ep"), split_axis=0, concat_axis=0, tiled=True)
    slice_width = summed.shape[2]
    route_rows = home_x.reshape(row_count, slice_width).astype(jnp.float32)
    d_tok = (
        jnp.zeros((tok_rows + 1, slice_width), jnp.float32)
        .at[token_of_slot]
        .add(route_rows)[:tok_rows]
    )
    d_probs = home_s.reshape(-1)[target].reshape(tok_rows, top_count)
    return (
        d_tok.astype(jnp.bfloat16),
        d_probs,
        grad_gate.astype(jnp.bfloat16)[None],
        grad_up.astype(jnp.bfloat16)[None],
        grad_down.astype(jnp.bfloat16)[None],
    )


def dense_device(tokens, out_grad, routes, probs, w_gate, w_up, w_down):
    owners = lax.axis_size(("role", "ep"))
    tok_rows, top_count = routes.shape
    part_width = w_gate.shape[2]
    experts = jnp.arange(owners, dtype=jnp.int32)
    chosen = routes[:, :, None] == experts[None, None, :]
    prob_table = jnp.sum(
        jnp.where(chosen, probs[:, :, None].astype(jnp.float32), 0.0), axis=1
    )
    send_p = prob_table.T.astype(jnp.bfloat16).reshape(owners, 1, tok_rows)
    recv_p = lax.all_to_all(send_p, ("role", "ep"), split_axis=0, concat_axis=0, tiled=True)
    weight_p = recv_p.reshape(owners * tok_rows, 1).astype(jnp.float32)
    rows_x = gather_rows(tokens)
    rows_g = gather_rows(out_grad)
    gate_up = jnp.concatenate([w_gate[0], w_up[0]], 1)
    down_shard = w_down[0]
    both_rows = jnp.dot(rows_x, gate_up, preferred_element_type=jnp.float32)
    gate_rows = both_rows[:, :part_width]
    up_rows = both_rows[:, part_width:]
    sigmoid_gate = jax.nn.sigmoid(gate_rows)
    activated = gate_rows * sigmoid_gate
    hidden = activated * up_rows
    back_rows = lax.dot_general(
        rows_g, down_shard, (((1,), (1,)), ((), ())), preferred_element_type=jnp.float32
    )
    scores = jnp.sum(hidden * back_rows, axis=1)
    hidden_grad = weight_p * back_rows
    d_gate_rows = (
        hidden_grad * up_rows * sigmoid_gate * (1.0 + gate_rows * (1.0 - sigmoid_gate))
    ).astype(jnp.bfloat16)
    d_up_rows = (hidden_grad * activated).astype(jnp.bfloat16)
    d_both = jnp.concatenate([d_gate_rows, d_up_rows], 1)
    scaled = (weight_p * hidden).astype(jnp.bfloat16)
    partial_low = lax.dot_general(
        d_both, gate_up, (((1,), (1,)), ((), ())), preferred_element_type=jnp.float32
    ).astype(jnp.bfloat16)
    summed = lax.psum_scatter(partial_low, ("role", "ep"), scatter_dimension=0, tiled=True)
    d_tok = lax.psum_scatter(summed, "tp", scatter_dimension=1, tiled=True)
    grad_down = lax.dot_general(
        scaled, rows_g, (((0,), (0,)), ((), ())), preferred_element_type=jnp.float32
    )
    grad_both = lax.dot_general(
        rows_x, d_both, (((0,), (0,)), ((), ())), preferred_element_type=jnp.float32
    )
    home_s = lax.all_to_all(
        scores.reshape(owners, 1, tok_rows), ("role", "ep"), split_axis=0, concat_axis=0, tiled=True
    )
    home_s = lax.psum(home_s, "tp").reshape(owners, tok_rows).T
    d_probs = jnp.sum(jnp.where(chosen, home_s[:, None, :], 0.0), axis=2)
    return (
        d_tok.astype(jnp.bfloat16),
        d_probs,
        grad_both[:, :part_width].astype(jnp.bfloat16)[None],
        grad_both[:, part_width:].astype(jnp.bfloat16)[None],
        grad_down.astype(jnp.bfloat16)[None],
    )


def gather_rows(block):
    wide = lax.all_gather(block, "tp", axis=1, tiled=True)
    return lax.all_gather(wide, ("role", "ep"), axis=0, tiled=True)


def per_device(*arrays):
    owners = lax.axis_size(("role", "ep"))
    if owners <= 2 * arrays[2].shape[1]:
        return dense_device(*arrays)
    return routed_device(*arrays)


def solution(mesh):
    in_specs = (
        P(("groups", "role", "ep"), "tp"),
        P(("groups", "role", "ep"), "tp"),
        P(("groups", "role", "ep"), None),
        P(("groups", "role", "ep"), None),
        P(("role", "ep"), None, "tp"),
        P(("role", "ep"), None, "tp"),
        P(("role", "ep"), "tp", None),
    )
    out_specs = (
        P(("groups", "role", "ep"), "tp"),
        P(("groups", "role", "ep"), None),
        P(("groups", "role", "ep"), None, "tp"),
        P(("groups", "role", "ep"), None, "tp"),
        P(("groups", "role", "ep"), "tp", None),
    )
    return jax.shard_map(
        per_device, mesh=mesh, in_specs=in_specs, out_specs=out_specs, check_vma=False
    )
```

```python
import jax
import jax.numpy as jnp
from jax import lax
from jax.sharding import PartitionSpec as P


def pad_rows(array):
    return jnp.concatenate([array, jnp.zeros((1, array.shape[1]), array.dtype)], 0)


def routed_device(tokens, out_grad, routes, probs, w_gate, w_up, w_down):
    owners = lax.axis_size(("role", "ep"))
    tok_rows, top_count = routes.shape
    width_full = w_gate.shape[1]
    part_width = w_gate.shape[2]
    capacity = min(tok_rows, tok_rows * top_count * 9 // (8 * owners))
    entry_total = tok_rows * top_count
    routes_flat = routes.reshape(-1)
    onehot = (routes_flat[:, None] == jnp.arange(owners, dtype=jnp.int32)[None, :]).astype(
        jnp.int32
    )
    before = jnp.cumsum(onehot, axis=0) - onehot
    slot_index = jnp.sum(before * onehot, axis=1)
    target = routes_flat * capacity + slot_index
    row_count = owners * capacity
    entry_of_slot = (
        jnp.full((row_count,), entry_total, jnp.int32)
        .at[target]
        .set(jnp.arange(entry_total, dtype=jnp.int32))
    )
    token_of_slot = entry_of_slot // top_count
    padded_prob = jnp.concatenate([probs.reshape(-1), jnp.zeros((1,), probs.dtype)], 0)
    send_prob = padded_prob[entry_of_slot].reshape(owners, capacity)
    send_x = pad_rows(tokens)[token_of_slot]
    send_g = pad_rows(out_grad)[token_of_slot]
    slice_x, slice_g, recv_p = (
        lax.all_to_all(
            send_x.reshape(owners, capacity, tokens.shape[1]),
            ("role", "ep"),
            split_axis=0,
            concat_axis=0,
            tiled=True,
        ),
        lax.all_to_all(
            send_g.reshape(owners, capacity, tokens.shape[1]),
            ("role", "ep"),
            split_axis=0,
            concat_axis=0,
            tiled=True,
        ),
        lax.all_to_all(send_prob, ("role", "ep"), split_axis=0, concat_axis=0, tiled=True),
    )
    recv_x, recv_g = (
        lax.all_gather(slice_x, "tp", axis=2, tiled=True),
        lax.all_gather(slice_g, "tp", axis=2, tiled=True),
    )
    rows_x = recv_x.reshape(row_count, width_full)
    rows_g = recv_g.reshape(row_count, width_full)
    weight_p = recv_p.reshape(row_count, 1).astype(jnp.float32)
    gate_up = jnp.concatenate([w_gate[0], w_up[0]], 1)
    down_shard = w_down[0]
    both_rows = jnp.dot(rows_x, gate_up, preferred_element_type=jnp.float32)
    gate_rows = both_rows[:, :part_width]
    up_rows = both_rows[:, part_width:]
    sigmoid_gate = jax.nn.sigmoid(gate_rows)
    activated = gate_rows * sigmoid_gate
    hidden = activated * up_rows
    back_rows = lax.dot_general(
        rows_g, down_shard, (((1,), (1,)), ((), ())), preferred_element_type=jnp.float32
    )
    scores = lax.psum(jnp.sum(hidden * back_rows, axis=1), "tp")
    hidden_grad = weight_p * back_rows
    d_gate_rows = (
        hidden_grad * up_rows * sigmoid_gate * (1.0 + gate_rows * (1.0 - sigmoid_gate))
    ).astype(jnp.bfloat16)
    d_up_rows = (hidden_grad * activated).astype(jnp.bfloat16)
    d_both = jnp.concatenate([d_gate_rows, d_up_rows], 1)
    scaled = (weight_p * hidden).astype(jnp.bfloat16)
    grad_down = lax.dot_general(
        scaled, rows_g, (((0,), (0,)), ((), ())), preferred_element_type=jnp.float32
    )
    grad_both = lax.dot_general(
        rows_x, d_both, (((0,), (0,)), ((), ())), preferred_element_type=jnp.float32
    )
    grad_gate = grad_both[:, :part_width]
    grad_up = grad_both[:, part_width:]
    partial_low = lax.dot_general(
        d_both, gate_up, (((1,), (1,)), ((), ())), preferred_element_type=jnp.float32
    ).astype(jnp.bfloat16)
    home_s = lax.all_to_all(
        scores.reshape(owners, capacity), ("role", "ep"), split_axis=0, concat_axis=0, tiled=True
    )
    summed = lax.psum_scatter(
        partial_low.reshape(owners, capacity, width_full), "tp", scatter_dimension=2, tiled=True
    ).astype(jnp.float32)
    summed_low = summed.astype(jnp.bfloat16)
    home_x = lax.all_to_all(summed_low, ("role", "ep"), split_axis=0, concat_axis=0, tiled=True)
    slice_width = summed.shape[2]
    route_rows = home_x.reshape(row_count, slice_width).astype(jnp.float32)
    d_tok = (
        jnp.zeros((tok_rows + 1, slice_width), jnp.float32)
        .at[token_of_slot]
        .add(route_rows)[:tok_rows]
    )
    d_probs = home_s.reshape(-1)[target].reshape(tok_rows, top_count)
    return (
        d_tok.astype(jnp.bfloat16),
        d_probs,
        grad_gate.astype(jnp.bfloat16)[None],
        grad_up.astype(jnp.bfloat16)[None],
        grad_down.astype(jnp.bfloat16)[None],
    )


def swap(block, axis):
    return lax.ppermute(block, axis, ((0, 1), (1, 0)))


def own_first(pair):
    return jnp.where(lax.axis_index("role") == 0, pair, pair[::-1])


def widen(block):
    other = swap(block, "tp")
    first = lax.axis_index("tp") == 0
    low = jnp.where(first, block, other)
    high = jnp.where(first, other, block)
    return jnp.concatenate([low, high], 1)


def half_rows(rows_x, rows_g, weight_p, gate_up, down_shard):
    part_width = down_shard.shape[0]
    both_rows = jnp.dot(rows_x, gate_up, preferred_element_type=jnp.float32)
    gate_rows = both_rows[:, :part_width]
    up_rows = both_rows[:, part_width:]
    sigmoid_gate = jax.nn.sigmoid(gate_rows)
    activated = gate_rows * sigmoid_gate
    hidden = activated * up_rows
    back_rows = lax.dot_general(
        rows_g, down_shard, (((1,), (1,)), ((), ())), preferred_element_type=jnp.float32
    )
    scores = jnp.sum(hidden * back_rows, axis=1)
    hidden_grad = weight_p * back_rows
    d_gate_rows = (
        hidden_grad * up_rows * sigmoid_gate * (1.0 + gate_rows * (1.0 - sigmoid_gate))
    ).astype(jnp.bfloat16)
    d_up_rows = (hidden_grad * activated).astype(jnp.bfloat16)
    d_both = jnp.concatenate([d_gate_rows, d_up_rows], 1)
    scaled = (weight_p * hidden).astype(jnp.bfloat16)
    partial_low = lax.dot_general(
        d_both, gate_up, (((1,), (1,)), ((), ())), preferred_element_type=jnp.float32
    ).astype(jnp.bfloat16)
    return scores, d_both, scaled, partial_low


def row_dot(left, right):
    return lax.dot_general(
        left, right, (((0,), (0,)), ((), ())), preferred_element_type=jnp.float32
    )


def dense_device(tokens, out_grad, routes, probs, w_gate, w_up, w_down):
    owners = lax.axis_size(("role", "ep"))
    tok_rows, top_count = routes.shape
    half_count = owners * tok_rows // 2
    slice_width = tokens.shape[1]
    part_width = w_gate.shape[2]
    experts = jnp.arange(owners, dtype=jnp.int32)
    chosen = routes[:, :, None] == experts[None, None, :]
    prob_table = jnp.sum(
        jnp.where(chosen, probs[:, :, None].astype(jnp.float32), 0.0), axis=1
    )
    own_x = lax.all_gather(widen(tokens), "ep", axis=0, tiled=True)
    send_p = prob_table.T.astype(jnp.bfloat16).reshape(owners, 1, tok_rows)
    recv_p = lax.all_to_all(send_p, ("role", "ep"), split_axis=0, concat_axis=0, tiled=True)
    recv_p, out_grad = lax.optimization_barrier((recv_p, out_grad))
    weight_p = own_first(recv_p.reshape(2, half_count)).astype(jnp.float32)
    own_g = lax.all_gather(widen(out_grad), "ep", axis=0, tiled=True)
    other_x = swap(own_x, "role")
    other_g = swap(own_g, "role")
    gate_up = jnp.concatenate([w_gate[0], w_up[0]], 1)
    down_shard = w_down[0]
    other_s, other_d, other_scaled, other_low = half_rows(
        other_x, other_g, weight_p[1][:, None], gate_up, down_shard
    )
    own_s, own_d, own_scaled, own_low = half_rows(
        own_x, own_g, weight_p[0][:, None], gate_up, down_shard
    )
    crossed = swap(other_low, "role")
    joined = (own_low.astype(jnp.float32) + crossed.astype(jnp.float32)).astype(jnp.bfloat16)
    scores, joined = lax.optimization_barrier((jnp.stack([own_s, other_s]), joined))
    summed = lax.psum_scatter(joined, "ep", scatter_dimension=0, tiled=True)
    first = lax.axis_index("tp") == 0
    low, high = summed[:, :slice_width], summed[:, slice_width:]
    kept = jnp.where(first, low, high).astype(jnp.float32)
    d_tok = kept + swap(jnp.where(first, high, low), "tp").astype(jnp.float32)
    grad_down = row_dot(own_scaled, own_g) + row_dot(other_scaled, other_g)
    grad_both = row_dot(own_x, own_d) + row_dot(other_x, other_d)
    home_s = lax.all_to_all(
        own_first(scores).reshape(owners, 1, tok_rows),
        ("role", "ep"),
        split_axis=0,
        concat_axis=0,
        tiled=True,
    )
    home_s = (home_s + swap(home_s, "tp")).reshape(owners, tok_rows).T
    d_probs = jnp.sum(jnp.where(chosen, home_s[:, None, :], 0.0), axis=2)
    return (
        d_tok.astype(jnp.bfloat16),
        d_probs,
        grad_both[:, :part_width].astype(jnp.bfloat16)[None],
        grad_both[:, part_width:].astype(jnp.bfloat16)[None],
        grad_down.astype(jnp.bfloat16)[None],
    )


def per_device(*arrays):
    owners = lax.axis_size(("role", "ep"))
    pairs = lax.axis_size("role") == 2 and lax.axis_size("tp") == 2
    if pairs and owners <= 2 * arrays[2].shape[1]:
        return dense_device(*arrays)
    return routed_device(*arrays)


def solution(mesh):
    in_specs = (
        P(("groups", "role", "ep"), "tp"),
        P(("groups", "role", "ep"), "tp"),
        P(("groups", "role", "ep"), None),
        P(("groups", "role", "ep"), None),
        P(("role", "ep"), None, "tp"),
        P(("role", "ep"), None, "tp"),
        P(("role", "ep"), "tp", None),
    )
    out_specs = (
        P(("groups", "role", "ep"), "tp"),
        P(("groups", "role", "ep"), None),
        P(("groups", "role", "ep"), None, "tp"),
        P(("groups", "role", "ep"), None, "tp"),
        P(("groups", "role", "ep"), "tp", None),
    )
    return jax.shard_map(
        per_device, mesh=mesh, in_specs=in_specs, out_specs=out_specs, check_vma=False
    )
```

```python
import jax
import jax.numpy as jnp
from jax import lax
from jax.sharding import PartitionSpec as P


def pad_rows(array):
    return jnp.concatenate([array, jnp.zeros((1, array.shape[1]), array.dtype)], 0)


def routed_device(tokens, out_grad, routes, probs, w_gate, w_up, w_down):
    owners = lax.axis_size(("role", "ep"))
    tok_rows, top_count = routes.shape
    width_full = w_gate.shape[1]
    part_width = w_gate.shape[2]
    capacity = min(tok_rows, tok_rows * top_count * 9 // (8 * owners))
    entry_total = tok_rows * top_count
    routes_flat = routes.reshape(-1)
    onehot = (routes_flat[:, None] == jnp.arange(owners, dtype=jnp.int32)[None, :]).astype(
        jnp.int32
    )
    before = jnp.cumsum(onehot, axis=0) - onehot
    slot_index = jnp.sum(before * onehot, axis=1)
    target = routes_flat * capacity + slot_index
    row_count = owners * capacity
    entry_of_slot = (
        jnp.full((row_count,), entry_total, jnp.int32)
        .at[target]
        .set(jnp.arange(entry_total, dtype=jnp.int32))
    )
    token_of_slot = entry_of_slot // top_count
    padded_prob = jnp.concatenate([probs.reshape(-1), jnp.zeros((1,), probs.dtype)], 0)
    send_prob = padded_prob[entry_of_slot].reshape(owners, capacity)
    send_x = pad_rows(tokens)[token_of_slot]
    send_g = pad_rows(out_grad)[token_of_slot]
    slice_x, slice_g, recv_p = (
        lax.all_to_all(
            send_x.reshape(owners, capacity, tokens.shape[1]),
            ("role", "ep"),
            split_axis=0,
            concat_axis=0,
            tiled=True,
        ),
        lax.all_to_all(
            send_g.reshape(owners, capacity, tokens.shape[1]),
            ("role", "ep"),
            split_axis=0,
            concat_axis=0,
            tiled=True,
        ),
        lax.all_to_all(send_prob, ("role", "ep"), split_axis=0, concat_axis=0, tiled=True),
    )
    recv_x, recv_g = (
        lax.all_gather(slice_x, "tp", axis=2, tiled=True),
        lax.all_gather(slice_g, "tp", axis=2, tiled=True),
    )
    rows_x = recv_x.reshape(row_count, width_full)
    rows_g = recv_g.reshape(row_count, width_full)
    weight_p = recv_p.reshape(row_count, 1).astype(jnp.float32)
    gate_up = jnp.concatenate([w_gate[0], w_up[0]], 1)
    down_shard = w_down[0]
    both_rows = jnp.dot(rows_x, gate_up, preferred_element_type=jnp.float32)
    gate_rows = both_rows[:, :part_width]
    up_rows = both_rows[:, part_width:]
    sigmoid_gate = jax.nn.sigmoid(gate_rows)
    activated = gate_rows * sigmoid_gate
    hidden = activated * up_rows
    back_rows = lax.dot_general(
        rows_g, down_shard, (((1,), (1,)), ((), ())), preferred_element_type=jnp.float32
    )
    scores = lax.psum(jnp.sum(hidden * back_rows, axis=1), "tp")
    hidden_grad = weight_p * back_rows
    d_gate_rows = (
        hidden_grad * up_rows * sigmoid_gate * (1.0 + gate_rows * (1.0 - sigmoid_gate))
    ).astype(jnp.bfloat16)
    d_up_rows = (hidden_grad * activated).astype(jnp.bfloat16)
    d_both = jnp.concatenate([d_gate_rows, d_up_rows], 1)
    scaled = (weight_p * hidden).astype(jnp.bfloat16)
    grad_down = lax.dot_general(
        scaled, rows_g, (((0,), (0,)), ((), ())), preferred_element_type=jnp.float32
    )
    grad_both = lax.dot_general(
        rows_x, d_both, (((0,), (0,)), ((), ())), preferred_element_type=jnp.float32
    )
    grad_gate = grad_both[:, :part_width]
    grad_up = grad_both[:, part_width:]
    partial_low = lax.dot_general(
        d_both, gate_up, (((1,), (1,)), ((), ())), preferred_element_type=jnp.float32
    ).astype(jnp.bfloat16)
    home_s = lax.all_to_all(
        scores.reshape(owners, capacity), ("role", "ep"), split_axis=0, concat_axis=0, tiled=True
    )
    summed = lax.psum_scatter(
        partial_low.reshape(owners, capacity, width_full), "tp", scatter_dimension=2, tiled=True
    ).astype(jnp.float32)
    summed_low = summed.astype(jnp.bfloat16)
    home_x = lax.all_to_all(summed_low, ("role", "ep"), split_axis=0, concat_axis=0, tiled=True)
    slice_width = summed.shape[2]
    route_rows = home_x.reshape(row_count, slice_width).astype(jnp.float32)
    d_tok = (
        jnp.zeros((tok_rows + 1, slice_width), jnp.float32)
        .at[token_of_slot]
        .add(route_rows)[:tok_rows]
    )
    d_probs = home_s.reshape(-1)[target].reshape(tok_rows, top_count)
    return (
        d_tok.astype(jnp.bfloat16),
        d_probs,
        grad_gate.astype(jnp.bfloat16)[None],
        grad_up.astype(jnp.bfloat16)[None],
        grad_down.astype(jnp.bfloat16)[None],
    )


def swap(block, axis):
    return lax.ppermute(block, axis, ((0, 1), (1, 0)))


def own_first(pair):
    return jnp.where(lax.axis_index("role") == 0, pair, pair[::-1])


def widen(block):
    other = swap(block, "tp")
    first = lax.axis_index("tp") == 0
    low = jnp.where(first, block, other)
    high = jnp.where(first, other, block)
    return jnp.concatenate([low, high], 1)


def ring_order(count):
    return list(range(0, count, 2)) + list(range(count - 1, 0, -2))


def ring_shift(block, step):
    count = lax.axis_size("ep")
    order = ring_order(count)
    return lax.ppermute(
        block, "ep", [(order[i], order[(i + step) % count]) for i in range(count)]
    )


def ring_gather(block, more_up):
    count = lax.axis_size("ep")
    up_steps = count // 2 if more_up else (count - 1) // 2
    blocks = {0: block}
    up, down = block, block
    for step in range(1, count // 2 + 1):
        if step <= up_steps:
            up = ring_shift(up, 1)
            blocks[count - step] = up
        if step <= count - 1 - up_steps:
            down = ring_shift(down, -1)
            blocks[step] = down
    return jnp.concatenate([blocks[i] for i in range(count)], 0)


def ring_scatter(rows):
    count = lax.axis_size("ep")
    blocks = rows.reshape(count, rows.shape[0] // count, rows.shape[1])
    half = rows.shape[1] // 2
    up, down = blocks[count - 1, :, :half], blocks[1 % count, :, half:]
    for step in range(1, count):
        up_next = blocks[count - 1 - step, :, :half].astype(jnp.float32)
        down_next = blocks[(1 + step) % count, :, half:].astype(jnp.float32)
        up = (ring_shift(up, 1).astype(jnp.float32) + up_next).astype(jnp.bfloat16)
        down = (ring_shift(down, -1).astype(jnp.float32) + down_next).astype(jnp.bfloat16)
    return jnp.concatenate([up, down], 1)


def half_rows(rows_x, rows_g, weight_p, gate_up, down_shard):
    part_width = down_shard.shape[0]
    both_rows = jnp.dot(rows_x, gate_up, preferred_element_type=jnp.float32)
    gate_rows = both_rows[:, :part_width]
    up_rows = both_rows[:, part_width:]
    sigmoid_gate = jax.nn.sigmoid(gate_rows)
    activated = gate_rows * sigmoid_gate
    hidden = activated * up_rows
    back_rows = lax.dot_general(
        rows_g, down_shard, (((1,), (1,)), ((), ())), preferred_element_type=jnp.float32
    )
    scores = jnp.sum(hidden * back_rows, axis=1)
    hidden_grad = weight_p * back_rows
    d_gate_rows = (
        hidden_grad * up_rows * sigmoid_gate * (1.0 + gate_rows * (1.0 - sigmoid_gate))
    ).astype(jnp.bfloat16)
    d_up_rows = (hidden_grad * activated).astype(jnp.bfloat16)
    d_both = jnp.concatenate([d_gate_rows, d_up_rows], 1)
    scaled = (weight_p * hidden).astype(jnp.bfloat16)
    partial_low = lax.dot_general(
        d_both, gate_up, (((1,), (1,)), ((), ())), preferred_element_type=jnp.float32
    ).astype(jnp.bfloat16)
    return scores, d_both, scaled, partial_low


def row_dot(left, right):
    return lax.dot_general(
        left, right, (((0,), (0,)), ((), ())), preferred_element_type=jnp.float32
    )


def dense_device(tokens, out_grad, routes, probs, w_gate, w_up, w_down):
    owners = lax.axis_size(("role", "ep"))
    tok_rows, top_count = routes.shape
    half_count = owners * tok_rows // 2
    slice_width = tokens.shape[1]
    part_width = w_gate.shape[2]
    experts = jnp.arange(owners, dtype=jnp.int32)
    chosen = routes[:, :, None] == experts[None, None, :]
    prob_table = jnp.sum(
        jnp.where(chosen, probs[:, :, None].astype(jnp.float32), 0.0), axis=1
    )
    own_x = ring_gather(widen(tokens), True)
    send_p = prob_table.T.astype(jnp.bfloat16).reshape(owners, 1, tok_rows)
    recv_p = lax.all_to_all(send_p, ("role", "ep"), split_axis=0, concat_axis=0, tiled=True)
    recv_p, out_grad = lax.optimization_barrier((recv_p, out_grad))
    count = owners // 2
    order = ring_order(count)
    place = [order.index(i) for i in range(count)]
    ring_at = jnp.array(place, jnp.int32)[lax.axis_index("ep")]
    to_ring = jnp.array(order, jnp.int32)[(ring_at + jnp.arange(count)) % count]
    from_ring = (jnp.array(place, jnp.int32) - ring_at + count) % count
    ring_p = recv_p.reshape(2, count, tok_rows)[:, to_ring]
    weight_p = own_first(ring_p.reshape(2, half_count)).astype(jnp.float32)
    own_g = ring_gather(widen(out_grad), False)
    other_x = swap(own_x, "role")
    other_g = swap(own_g, "role")
    gate_up = jnp.concatenate([w_gate[0], w_up[0]], 1)
    down_shard = w_down[0]
    other_s, other_d, other_scaled, other_low = half_rows(
        other_x, other_g, weight_p[1][:, None], gate_up, down_shard
    )
    own_s, own_d, own_scaled, own_low = half_rows(
        own_x, own_g, weight_p[0][:, None], gate_up, down_shard
    )
    crossed = swap(other_low, "role")
    joined = (own_low.astype(jnp.float32) + crossed.astype(jnp.float32)).astype(jnp.bfloat16)
    scores, joined = lax.optimization_barrier((jnp.stack([own_s, other_s]), joined))
    summed = ring_scatter(joined)
    first = lax.axis_index("tp") == 0
    low, high = summed[:, :slice_width], summed[:, slice_width:]
    kept = jnp.where(first, low, high).astype(jnp.float32)
    d_tok = kept + swap(jnp.where(first, high, low), "tp").astype(jnp.float32)
    grad_down = row_dot(own_scaled, own_g) + row_dot(other_scaled, other_g)
    grad_both = row_dot(own_x, own_d) + row_dot(other_x, other_d)
    home_s = lax.all_to_all(
        own_first(scores).reshape(2, count, tok_rows)[:, from_ring].reshape(owners, 1, tok_rows),
        ("role", "ep"),
        split_axis=0,
        concat_axis=0,
        tiled=True,
    )
    home_s = (home_s + swap(home_s, "tp")).reshape(owners, tok_rows).T
    d_probs = jnp.sum(jnp.where(chosen, home_s[:, None, :], 0.0), axis=2)
    return (
        d_tok.astype(jnp.bfloat16),
        d_probs,
        grad_both[:, :part_width].astype(jnp.bfloat16)[None],
        grad_both[:, part_width:].astype(jnp.bfloat16)[None],
        grad_down.astype(jnp.bfloat16)[None],
    )


def per_device(*arrays):
    owners = lax.axis_size(("role", "ep"))
    pairs = lax.axis_size("role") == 2 and lax.axis_size("tp") == 2
    if pairs and owners <= 2 * arrays[2].shape[1]:
        return dense_device(*arrays)
    return routed_device(*arrays)


def solution(mesh):
    in_specs = (
        P(("groups", "role", "ep"), "tp"),
        P(("groups", "role", "ep"), "tp"),
        P(("groups", "role", "ep"), None),
        P(("groups", "role", "ep"), None),
        P(("role", "ep"), None, "tp"),
        P(("role", "ep"), None, "tp"),
        P(("role", "ep"), "tp", None),
    )
    out_specs = (
        P(("groups", "role", "ep"), "tp"),
        P(("groups", "role", "ep"), None),
        P(("groups", "role", "ep"), None, "tp"),
        P(("groups", "role", "ep"), None, "tp"),
        P(("groups", "role", "ep"), "tp", None),
    )
    return jax.shard_map(
        per_device, mesh=mesh, in_specs=in_specs, out_specs=out_specs, check_vma=False
    )
```
